32 devices in a mesh: dp: 16 (over z, y, core), mp: 2 (over x).
Axes of the slice: x: 2, y: 2, z: 4, core: 2. Of those that a mesh axis runs over, the one named last changes fastest.
Arguments:
- frames: bfloat16 [512, 16, 1024], P(('dp', 'mp')), may hold values from -6 to 6
- offsets: int32 [512, 16], P(('dp', 'mp')), may hold values from 1 to 2
- gain_attn: float32 [16, 1024], replicated, may hold values from 0.25 to 1.75
- w_qkv: bfloat16 [16, 3, 1024, 1024], P(None, None, 'dp', 'mp'), may hold values from -0.1875 to 0.1875
- w_out: bfloat16 [16, 1024, 1024], P(None, 'mp', 'dp'), may hold values from -0.375 to 0.375
- gain_ffn: float32 [16, 1024], replicated, may hold values from 0.25 to 1.75
- w_gu: bfloat16 [16, 2, 1024, 4096], P(None, None, 'dp', 'mp'), may hold values from -0.1875 to 0.1875
- w_down: bfloat16 [16, 4096, 1024], P(None, 'mp', 'dp'), may hold values from -0.1875 to 0.1875
- cotangent: bfloat16 [512, 16, 1024], P(('dp', 'mp')), may hold values from -6 to 6
Outputs:
- result: bfloat16 [512, 16, 1024], P(('dp', 'mp'))
- grad_frames: bfloat16 [512, 16, 1024], P(('dp', 'mp'))
- grad_gain_attn: float32 [16, 1024], P(None, ('dp', 'mp'))
- grad_w_qkv: float32 [16, 3, 1024, 1024], P(None, None, 'dp', 'mp')
- grad_w_out: float32 [16, 1024, 1024], P(None, 'mp', 'dp')
- grad_gain_ffn: float32 [16, 1024], P(None, ('dp', 'mp'))
- grad_w_gu: float32 [16, 2, 1024, 4096], P(None, None, 'dp', 'mp')
- grad_w_down: float32 [16, 4096, 1024], P(None, 'mp', 'dp')
The draws below stay inside these ranges and needn't reach their ends.
All inputs are finite; a program needn't handle non-finite values.
Results may differ from the reference program's by a relative error of at most 0.02.
Values may be sent and summed in bfloat16 or wider, within the bound.
No kernel may reach another device: no remote copies, remote signals or barrier semaphores. Data moves between devices by JAX's collectives and lax.ppermute only.
A program may use at most 640 MiB of HBM per device.

```python
import math
import jax
import jax.numpy as jnp
from jax import lax

D = 1024
HEADS = 16
HD = 64
FF = 4096
P_SIZE = 16
FRAMES = 512


def with_ends(array, key, low, largest):
    spot = [jax.random.randint(jax.random.fold_in(key, axis), (), 0, length) for axis, length in enumerate(array.shape)]
    longest = array.shape.index(max(array.shape))
    neighbour = spot[:longest] + [(spot[longest] + 1) % array.shape[longest]] + spot[longest + 1:]
    return array.at[tuple(spot)].set(low).at[tuple(neighbour)].set(largest)


def with_spikes(array, own_key, source, target, parts, factor):
    owner, partner = [(jnp.arange(array.shape[position]) // (array.shape[position] // parts)).reshape([-1 if axis == position else 1 for axis in range(array.ndim)]) for position in (source, target)]
    chosen = jax.random.permutation(own_key, parts)[partner]
    strong = (owner == chosen) | (owner == (partner + parts // 2) % parts)
    return jnp.where(strong, factor * array, array)


def block_scale(key, dims, split, least, largest):
    def one(axis_at, blocks):
        steps = jax.random.uniform(jax.random.fold_in(jax.random.fold_in(key, 6), axis_at), (blocks,), jnp.float32, least / len(split), largest / len(split))
        return jnp.repeat(jnp.exp(steps), dims[axis_at] // blocks).reshape((-1,) + (1,) * (len(dims) - axis_at - 1))

    gain = one(*split[0])
    for cut in split[1:]:
        gain = gain * one(*cut)
    return gain


def bell_draw(rng, shape, width, limit, split=(), dtype=jnp.bfloat16):
    loudness = block_scale(rng, shape, split, -0.22, 0.18) if split else 1.0
    array = jax.random.normal(rng, shape, jnp.float32) * width * loudness
    return jnp.minimum(jnp.maximum(array, -limit), limit).astype(dtype)


def bell_draw_with(own_key, dims, scale, reach, cuts, heavy, held_as=jnp.bfloat16):
    values = scale * jax.random.normal(own_key, dims, jnp.float32)
    if cuts:
        values = values * block_scale(own_key, dims, cuts, -0.22, 0.18)
    return jnp.clip(with_spikes(values, jax.random.fold_in(own_key, 3), *heavy), -reach, reach).astype(held_as)


def setup_inputs(seed: int = 0) -> dict:
    streams_of = jax.random.split(jax.random.key(seed), 10)
    return {
        "frames": bell_draw(streams_of[0], (FRAMES, P_SIZE, D), 1.0, 6.0, ((0, 32),)),
        "offsets": with_ends(jax.random.randint(streams_of[1], (FRAMES, P_SIZE), 1, 3), jax.random.fold_in(streams_of[1], 1), 1, 2).astype(jnp.int32),
        "gain_attn": jnp.clip(1.0 + 0.15 * jax.random.normal(streams_of[2], (P_SIZE, D), jnp.float32), 0.25, 1.75),
        "w_qkv": bell_draw(streams_of[3], (P_SIZE, 3, D, HEADS * HD), D ** -0.5, 0.1875, ((2, 16), (3, 2))),
        "w_out": bell_draw(streams_of[4], (P_SIZE, HEADS * HD, D), (HEADS * HD // 4) ** -0.5, 0.375, ((1, 2), (2, 16))),
        "gain_ffn": jnp.clip(1.0 + 0.15 * jax.random.normal(streams_of[5], (P_SIZE, D), jnp.float32), 0.25, 1.75),
        "w_gu": bell_draw(streams_of[6], (P_SIZE, 2, D, FF), D ** -0.5, 0.1875, ((2, 16), (3, 2))),
        "w_down": bell_draw(streams_of[7], (P_SIZE, FF, D), (FF // 4) ** -0.5, 0.1875, ((1, 2), (2, 16))),
        "cotangent": bell_draw_with(streams_of[8], (FRAMES, P_SIZE, D), 1.0, 6.0, ((0, 32),), (0, 2, 32, 2.75)),
    }


@jax.custom_vjp
def low(v):
    return lax.optimization_barrier(v.astype(jnp.bfloat16)).astype(jnp.float32)

@jax.custom_vjp
def low_back(v):
    return v

def low_keep(v):
    return (low(v), None)

def low_pass(kept, grad):
    return (grad,)

def back_keep(v):
    return (v, None)

def back_low(kept, grad):
    return (low(grad),)
low.defvjp(low_keep, low_pass)
low_back.defvjp(back_keep, back_low)
norm_eps = 1e-06
highest = lax.Precision.HIGHEST

def rms_scale(residual, norm_gain):
    scaling = lax.rsqrt(lax.optimization_barrier(jnp.mean(residual * residual, axis=-1, keepdims=True)) + norm_eps)
    return residual * scaling * norm_gain

def block_forward(residual, gain_attn, w_qkv, w_out, gain_ffn, w_gu, w_down):
    frame_count = residual.shape[0]
    positions = residual.shape[1]
    normed = low(rms_scale(residual, gain_attn))
    qkv = low_back(low(jnp.einsum('fpd,pjde->fpje', normed, w_qkv, precision=highest)))
    queries = qkv[:, :, 0].reshape(frame_count, positions, HEADS, HD)
    key_rows = qkv[:, :, 1].reshape(frame_count, positions, HEADS, HD)
    value_rows = qkv[:, :, 2].reshape(frame_count, positions, HEADS, HD)
    scores = low_back(jnp.einsum('fphe,fqhe->fhpq', queries, key_rows, precision=highest) * HD ** (-0.5))
    causal = jnp.arange(positions)[:, None] >= jnp.arange(positions)[None, :]
    scores = jnp.where(causal, scores, -1e+30)
    row_max = lax.optimization_barrier(jnp.max(scores, axis=-1, keepdims=True))
    exp_scores = jnp.exp(scores - row_max)
    attn_probs = low(exp_scores / lax.optimization_barrier(jnp.sum(exp_scores, axis=-1, keepdims=True)))
    mixed = jnp.einsum('fhpq,fqhe->fphe', attn_probs, value_rows, precision=highest)
    mixed = low_back(low(mixed.reshape(frame_count, positions, HEADS * HD)))
    attn_branch = low_back(jnp.einsum('fpe,ped->fpd', mixed, w_out, precision=highest))
    hidden_in = residual + attn_branch
    normed_two = low(rms_scale(hidden_in, gain_ffn))
    gate_up = low_back(jnp.einsum('fpd,pjde->fpje', normed_two, w_gu, precision=highest))
    gate_pre = gate_up[:, :, 0]
    hidden = low(gate_pre * jax.nn.sigmoid(gate_pre) * gate_up[:, :, 1])
    ffn_branch = low_back(jnp.einsum('fpe,ped->fpd', hidden, w_down, precision=highest))
    return hidden_in + ffn_branch

def reference(frames, offsets, gain_attn, w_qkv, w_out, gain_ffn, w_gu, w_down, cotangent):
    frame_total = frames.shape[0]
    block_rows = math.gcd(frame_total, 256)

    def forward(frames_wide, gain_one, wide_qkv, wide_out, gain_two, wide_gu, wide_down):
        padded = jnp.pad(frames_wide, ((2, 0), (0, 0), (0, 0)))
        residual = jnp.where((offsets == 1)[:, :, None], padded[1:frame_total + 1], padded[0:frame_total])
        grouped = residual.reshape(frame_total // block_rows, block_rows, residual.shape[1], residual.shape[2])
        stepper = jax.checkpoint(lambda segment: block_forward(segment, gain_one, wide_qkv, wide_out, gain_two, wide_gu, wide_down))
        return lax.map(stepper, grouped).reshape(residual.shape)
    primals = (frames.astype(jnp.float32), gain_attn, w_qkv.astype(jnp.float32), w_out.astype(jnp.float32), gain_ffn, w_gu.astype(jnp.float32), w_down.astype(jnp.float32))
    result, pullback = jax.vjp(forward, *primals)
    gradients = pullback(cotangent.astype(jnp.float32))
    return (result.astype(jnp.bfloat16), gradients[0].astype(jnp.bfloat16), gradients[1], gradients[2], gradients[3], gradients[4], gradients[5], gradients[6])
```

```python
import jax
import jax.numpy as jnp
from jax import lax
from jax.sharding import PartitionSpec as P

HD = 64


norm_eps = 1e-06


def from_behind(value, axis, steps):
    count = lax.axis_size(axis)
    initial, last = (max(0, -steps), min(count, count - steps))
    return lax.ppermute(value, axis, [(source, source + steps) for source in range(initial, last)])


def delayed(frames, offsets):
    prior = from_behind(frames[-2:], ("dp", "mp"), 1)
    joined = jnp.concatenate([prior, frames], axis=0).astype(jnp.float32)
    row_count = frames.shape[0]
    return jnp.where((offsets == 1)[:, :, None], joined[1 : row_count + 1], joined[0:row_count])


def normalize(residual, norm_gain):
    scaling = lax.rsqrt(jnp.mean(residual * residual, axis=-1, keepdims=True) + norm_eps)
    unit_rows = residual * scaling
    return (unit_rows, scaling, (unit_rows * norm_gain).astype(jnp.bfloat16))


def norm_back(grad_normed, unit_rows, scaling, norm_gain):
    weighted = grad_normed * norm_gain
    inner_mean = jnp.mean(weighted * unit_rows, axis=-1, keepdims=True)
    return (scaling * (weighted - unit_rows * inner_mean), jnp.sum(grad_normed * unit_rows, axis=0))


def head_scores(qkv_low, head_width):
    frame_count = qkv_low.shape[0]
    positions = qkv_low.shape[1]
    head_count = qkv_low.shape[3] // head_width
    queries = qkv_low[:, :, 0].reshape(frame_count, positions, head_count, head_width)
    key_rows = qkv_low[:, :, 1].reshape(frame_count, positions, head_count, head_width)
    value_rows = qkv_low[:, :, 2].reshape(frame_count, positions, head_count, head_width)
    scaling = head_width ** (-0.5)
    scores = (
        jnp.einsum("fphe,fqhe->fhpq", queries, key_rows, preferred_element_type=jnp.float32)
        * scaling
    )
    causal = jnp.arange(positions)[:, None] >= jnp.arange(positions)[None, :]
    scores = jnp.where(causal, scores, -1e30)
    return (queries, key_rows, value_rows, scores, scaling)


def attend(qkv_low, head_width):
    queries, key_rows, value_rows, scores, scaling = head_scores(qkv_low, head_width)
    row_max = jnp.max(scores, axis=-1, keepdims=True)
    log_total = row_max + jnp.log(jnp.sum(jnp.exp(scores - row_max), axis=-1, keepdims=True))
    probs_low = jnp.exp(scores - log_total).astype(jnp.bfloat16)
    mixed = jnp.einsum("fhpq,fqhe->fphe", probs_low, value_rows, preferred_element_type=jnp.float32)
    mixed_low = mixed.reshape(qkv_low.shape[0], qkv_low.shape[1], qkv_low.shape[3]).astype(
        jnp.bfloat16
    )
    return (mixed_low, log_total)


def attend_back(qkv_low, grad_mixed, log_total, head_width):
    queries, key_rows, value_rows, scores, scaling = head_scores(qkv_low, head_width)
    attn_probs = jnp.exp(scores - log_total)
    probs_low = attn_probs.astype(jnp.bfloat16)
    grad_heads = grad_mixed.reshape(queries.shape)
    grad_values = jnp.einsum(
        "fhpq,fphe->fqhe", probs_low, grad_heads, preferred_element_type=jnp.float32
    )
    grad_probs = jnp.einsum(
        "fphe,fqhe->fhpq", grad_heads, value_rows, preferred_element_type=jnp.float32
    )
    row_inner = jnp.sum(attn_probs * grad_probs, axis=-1, keepdims=True)
    grad_scores = (attn_probs * (grad_probs - row_inner)).astype(jnp.bfloat16)
    grad_queries = (
        jnp.einsum("fhpq,fqhe->fphe", grad_scores, key_rows, preferred_element_type=jnp.float32)
        * scaling
    )
    grad_keys = (
        jnp.einsum("fhpq,fphe->fqhe", grad_scores, queries, preferred_element_type=jnp.float32)
        * scaling
    )
    stacked = jnp.stack([grad_queries, grad_keys, grad_values], axis=2)
    return stacked.reshape(qkv_low.shape).astype(jnp.bfloat16)


def swap(value):
    return lax.all_to_all(value, "dp", split_axis=0, concat_axis=0, tiled=True)


def weights_to_positions(shards):
    copies = lax.axis_size("dp") // shards.shape[0]
    return swap(jnp.repeat(shards, copies, axis=0) if copies > 1 else shards)


def grads_to_shards(blocks, positions):
    arrived = swap(blocks.astype(jnp.bfloat16))
    copies = arrived.shape[0] // positions
    parts = arrived.reshape(positions, copies, *arrived.shape[1:]).astype(jnp.float32)
    return jnp.sum(parts, axis=1) if copies > 1 else parts[:, 0]


def rows_to_positions(value):
    frame_count, positions, width = value.shape
    count = lax.axis_size("dp")
    copies = count // positions
    part = frame_count // copies
    split = value.reshape(copies, part, positions, width).transpose(2, 0, 1, 3)
    return swap(split.reshape(count, part, width))


def rows_to_frames(value, positions):
    arrived = swap(value)
    count, part, width = arrived.shape
    copies = count // positions
    split = arrived.reshape(positions, copies, part, width).transpose(1, 2, 0, 3)
    return split.reshape(copies * part, positions, width)


def both(value):
    return lax.all_gather(value, "mp", axis=0, tiled=True)


def matmul(left, right, spec):
    return jnp.einsum(spec, left, right, preferred_element_type=jnp.float32)


def body(frames, offsets, gain_attn, w_qkv, w_out, gain_ffn, w_gu, w_down, cotangent):
    row_count, positions, width = frames.shape
    count = lax.axis_size("dp")
    groups = lax.axis_size("mp")
    copies = count // positions
    part = row_count // copies
    mine = lax.axis_index("dp") // copies
    attn_gain = lax.dynamic_index_in_dim(gain_attn, mine, 0, keepdims=False)
    ffn_gain = lax.dynamic_index_in_dim(gain_ffn, mine, 0, keepdims=False)
    heads_width = w_qkv.shape[3]
    units = w_gu.shape[3]

    def flat(value):
        return value.reshape(-1, value.shape[-1])

    def own_sum(value):
        return lax.psum_scatter(
            value.reshape(groups * count, part, width), "mp", scatter_dimension=0, tiled=True
        ).astype(jnp.float32)

    def to_heads(value):
        split = value.reshape(groups, count, part, -1).transpose(1, 0, 2, 3)
        return rows_to_frames(split.reshape(count, groups * part, -1), positions)

    resid_bf = delayed(frames, offsets).astype(jnp.bfloat16)
    resid_in = rows_to_positions(resid_bf).astype(jnp.float32)
    cot_own = rows_to_positions(cotangent)
    unit_one, scale_one, normed_one = normalize(resid_in, attn_gain)
    group_norm = flat(both(normed_one))
    group_cot = flat(both(cot_own))
    full_qkv = weights_to_positions(w_qkv).transpose(1, 0, 2, 3).reshape(3, width, heads_width)
    full_out = weights_to_positions(w_out.transpose(0, 2, 1)).reshape(width, heads_width)
    full_gu = weights_to_positions(w_gu).transpose(1, 0, 2, 3).reshape(2, width, units)
    full_down = weights_to_positions(w_down.transpose(0, 2, 1)).reshape(width, units)

    qkv_pos = matmul(group_norm, full_qkv, "xd,jde->xje").astype(jnp.bfloat16)
    qkv_low = to_heads(qkv_pos).reshape(copies * groups * part, positions, 3, heads_width)
    mixed_low, log_total = attend(qkv_low, HD)

    def frames_to_rows(value):
        moved = rows_to_positions(value)
        split = moved.reshape(count, groups, part, -1).transpose(1, 0, 2, 3)
        return split.reshape(groups * count * part, -1)

    mixed_pos = frames_to_rows(mixed_low)
    attn_sum = own_sum(matmul(mixed_pos, full_out, "xe,de->xd"))
    hidden_in = resid_in + attn_sum
    unit_two, scale_two, normed_two = normalize(hidden_in, ffn_gain)
    group_two = flat(both(normed_two))
    gate_up = matmul(group_two, full_gu, "xd,jde->jxe")
    gate_pre = gate_up[0]
    up_pre = gate_up[1]
    sigmoid_gate = jax.nn.sigmoid(gate_pre)
    silu_gate = gate_pre * sigmoid_gate
    hidden_low = (silu_gate * up_pre).astype(jnp.bfloat16)
    ffn_sum = own_sum(matmul(hidden_low, full_down, "xe,de->xd").astype(jnp.bfloat16))
    result = rows_to_frames((hidden_in + ffn_sum).astype(jnp.bfloat16), positions)

    grad_down = matmul(group_cot, hidden_low, "xd,xe->de")
    grad_hidden = matmul(group_cot, full_down, "xd,de->xe")
    slope = sigmoid_gate * (1.0 + gate_pre * (1.0 - sigmoid_gate))
    grad_gu = jnp.stack([grad_hidden * up_pre * slope, grad_hidden * silu_gate]).astype(
        jnp.bfloat16
    )
    grad_wgu = matmul(group_two, grad_gu, "xd,jxe->jde")
    grad_normed_two = own_sum(matmul(grad_gu, full_gu, "jxe,jde->xd").astype(jnp.bfloat16))
    back_two, gain_two = norm_back(grad_normed_two, unit_two, scale_two, ffn_gain)
    grad_hidden_in = cot_own.astype(jnp.float32) + back_two
    group_grad = flat(both(grad_hidden_in.astype(jnp.bfloat16)))
    grad_wout = matmul(group_grad, mixed_pos, "xd,xe->de")
    grad_mixed = matmul(group_grad, full_out, "xd,de->xe").astype(jnp.bfloat16)
    grad_mixed_low = to_heads(grad_mixed)
    grad_qkv_low = attend_back(qkv_low, grad_mixed_low, log_total, HD)
    grad_qkv = frames_to_rows(
        grad_qkv_low.reshape(copies * groups * part, positions, 3 * heads_width)
    ).reshape(-1, 3, heads_width)
    grad_wqkv = matmul(group_norm, grad_qkv, "xd,xje->jde")
    grad_normed_one = own_sum(matmul(grad_qkv, full_qkv, "xje,jde->xd").astype(jnp.bfloat16))
    back_one, gain_one = norm_back(grad_normed_one, unit_one, scale_one, attn_gain)
    grad_resid = rows_to_frames((grad_hidden_in + back_one).astype(jnp.bfloat16), positions).astype(
        jnp.float32
    )
    one_step = jnp.where((offsets == 1)[:, :, None], grad_resid, 0.0)
    two_step = jnp.where((offsets == 2)[:, :, None], grad_resid, 0.0)
    spread = jnp.pad(one_step, ((1, 1), (0, 0), (0, 0))) + jnp.pad(
        two_step, ((0, 2), (0, 0), (0, 0))
    )
    returned = from_behind(spread[:2].astype(jnp.bfloat16), ("dp", "mp"), -1).astype(jnp.float32)
    grad_frames = (spread[2:] + jnp.pad(returned, ((row_count - 2, 0), (0, 0), (0, 0)))).astype(
        jnp.bfloat16
    )
    gains = jnp.stack([jnp.sum(gain_one, axis=0), jnp.sum(gain_two, axis=0)])
    gains = gains.reshape(2, count, groups, width // (count * groups))
    gains = lax.psum_scatter(
        gains.transpose(2, 1, 0, 3), "mp", scatter_dimension=0, tiled=False
    )
    gains = swap(gains)
    gains = jnp.sum(gains.reshape(positions, copies, 2, -1), axis=1)

    def split_rows(value):
        stacked = value.shape[0]
        return value.reshape(stacked, count, width // count, -1).transpose(1, 0, 2, 3)

    shard_qkv = grads_to_shards(split_rows(grad_wqkv), positions)
    shard_out = grads_to_shards(grad_wout.reshape(count, -1, heads_width), positions)
    shard_gu = grads_to_shards(split_rows(grad_wgu), positions)
    shard_down = grads_to_shards(grad_down.reshape(count, -1, units), positions)
    return (
        result,
        grad_frames,
        gains[:, 0],
        shard_qkv,
        shard_out.transpose(0, 2, 1),
        gains[:, 1],
        shard_gu,
        shard_down.transpose(0, 2, 1),
    )


def solution(mesh):
    return jax.shard_map(
        body,
        mesh=mesh,
        in_specs=(
            P(("dp", "mp"), None, None),
            P(("dp", "mp"), None),
            P(),
            P(None, None, "dp", "mp"),
            P(None, "mp", "dp"),
            P(),
            P(None, None, "dp", "mp"),
            P(None, "mp", "dp"),
            P(("dp", "mp"), None, None),
        ),
        out_specs=(
            P(("dp", "mp"), None, None),
            P(("dp", "mp"), None, None),
            P(None, ("dp", "mp")),
            P(None, None, "dp", "mp"),
            P(None, "mp", "dp"),
            P(None, ("dp", "mp")),
            P(None, None, "dp", "mp"),
            P(None, "mp", "dp"),
        ),
        check_vma=False,
    )
```

```python
import jax
import jax.numpy as jnp
from jax import lax
from jax.sharding import PartitionSpec as P

HD = 64


norm_eps = 1e-06


def from_behind(value, axis, steps):
    count = lax.axis_size(axis)
    initial, last = (max(0, -steps), min(count, count - steps))
    return lax.ppermute(value, axis, [(source, source + steps) for source in range(initial, last)])


def delayed(frames, offsets):
    prior = from_behind(frames[-2:], ("dp", "mp"), 1)
    joined = jnp.concatenate([prior, frames], axis=0).astype(jnp.float32)
    row_count = frames.shape[0]
    return jnp.where((offsets == 1)[:, :, None], joined[1 : row_count + 1], joined[0:row_count])


def normalize(residual, norm_gain):
    scaling = lax.rsqrt(jnp.mean(residual * residual, axis=-1, keepdims=True) + norm_eps)
    unit_rows = residual * scaling
    return (unit_rows, scaling, (unit_rows * norm_gain).astype(jnp.bfloat16))


def norm_back(grad_normed, unit_rows, scaling, norm_gain):
    weighted = grad_normed * norm_gain
    inner_mean = jnp.mean(weighted * unit_rows, axis=-1, keepdims=True)
    return (scaling * (weighted - unit_rows * inner_mean), jnp.sum(grad_normed * unit_rows, axis=0))


def head_scores(qkv_low, head_width):
    frame_count = qkv_low.shape[0]
    positions = qkv_low.shape[1]
    head_count = qkv_low.shape[3] // head_width
    queries = qkv_low[:, :, 0].reshape(frame_count, positions, head_count, head_width)
    key_rows = qkv_low[:, :, 1].reshape(frame_count, positions, head_count, head_width)
    value_rows = qkv_low[:, :, 2].reshape(frame_count, positions, head_count, head_width)
    scaling = head_width ** (-0.5)
    scores = (
        jnp.einsum("fphe,fqhe->fhpq", queries, key_rows, preferred_element_type=jnp.float32)
        * scaling
    )
    causal = jnp.arange(positions)[:, None] >= jnp.arange(positions)[None, :]
    scores = jnp.where(causal, scores, -1e30)
    return (queries, key_rows, value_rows, scores, scaling)


def attend(qkv_low, head_width):
    queries, key_rows, value_rows, scores, scaling = head_scores(qkv_low, head_width)
    row_max = jnp.max(scores, axis=-1, keepdims=True)
    log_total = row_max + jnp.log(jnp.sum(jnp.exp(scores - row_max), axis=-1, keepdims=True))
    probs_low = jnp.exp(scores - log_total).astype(jnp.bfloat16)
    mixed = jnp.einsum("fhpq,fqhe->fphe", probs_low, value_rows, preferred_element_type=jnp.float32)
    mixed_low = mixed.reshape(qkv_low.shape[0], qkv_low.shape[1], qkv_low.shape[3]).astype(
        jnp.bfloat16
    )
    return (mixed_low, log_total)


def attend_back(qkv_low, grad_mixed, log_total, head_width):
    queries, key_rows, value_rows, scores, scaling = head_scores(qkv_low, head_width)
    attn_probs = jnp.exp(scores - log_total)
    probs_low = attn_probs.astype(jnp.bfloat16)
    grad_heads = grad_mixed.reshape(queries.shape)
    grad_values = jnp.einsum(
        "fhpq,fphe->fqhe", probs_low, grad_heads, preferred_element_type=jnp.float32
    )
    grad_probs = jnp.einsum(
        "fphe,fqhe->fhpq", grad_heads, value_rows, preferred_element_type=jnp.float32
    )
    row_inner = jnp.sum(attn_probs * grad_probs, axis=-1, keepdims=True)
    grad_scores = (attn_probs * (grad_probs - row_inner)).astype(jnp.bfloat16)
    grad_queries = (
        jnp.einsum("fhpq,fqhe->fphe", grad_scores, key_rows, preferred_element_type=jnp.float32)
        * scaling
    )
    grad_keys = (
        jnp.einsum("fhpq,fphe->fqhe", grad_scores, queries, preferred_element_type=jnp.float32)
        * scaling
    )
    stacked = jnp.stack([grad_queries, grad_keys, grad_values], axis=2)
    return stacked.reshape(qkv_low.shape).astype(jnp.bfloat16)


def swap(value):
    return lax.all_to_all(value, "dp", split_axis=0, concat_axis=0, tiled=True)


def weights_to_positions(shards):
    copies = lax.axis_size("dp") // shards.shape[0]
    return swap(jnp.repeat(shards, copies, axis=0) if copies > 1 else shards)


def grads_to_shards(blocks, positions):
    return sum_arrived(swap(blocks.astype(jnp.bfloat16)), positions)


def sum_arrived(arrived, positions):
    copies = arrived.shape[0] // positions
    parts = arrived.reshape(positions, copies, *arrived.shape[1:]).astype(jnp.float32)
    return jnp.sum(parts, axis=1) if copies > 1 else parts[:, 0]


def rows_to_positions(value):
    frame_count, positions, width = value.shape
    count = lax.axis_size("dp")
    copies = count // positions
    part = frame_count // copies
    split = value.reshape(copies, part, positions, width).transpose(2, 0, 1, 3)
    return swap(split.reshape(count, part, width))


def rows_to_frames(value, positions):
    arrived = swap(value)
    count, part, width = arrived.shape
    copies = count // positions
    split = arrived.reshape(positions, copies, part, width).transpose(1, 2, 0, 3)
    return split.reshape(copies * part, positions, width)


def both(value):
    return lax.all_gather(value, "mp", axis=0, tiled=True)


def matmul(left, right, spec):
    return jnp.einsum(spec, left, right, preferred_element_type=jnp.float32)


def body(frames, offsets, gain_attn, w_qkv, w_out, gain_ffn, w_gu, w_down, cotangent):
    row_count, positions, width = frames.shape
    count = lax.axis_size("dp")
    groups = lax.axis_size("mp")
    copies = count // positions
    part = row_count // copies
    mine = lax.axis_index("dp") // copies
    attn_gain = lax.dynamic_index_in_dim(gain_attn, mine, 0, keepdims=False)
    ffn_gain = lax.dynamic_index_in_dim(gain_ffn, mine, 0, keepdims=False)
    heads_width = w_qkv.shape[3]
    units = w_gu.shape[3]

    def flat(value):
        return value.reshape(-1, value.shape[-1])

    def own_sum(value):
        return lax.psum_scatter(
            value.reshape(groups * count, part, width), "mp", scatter_dimension=0, tiled=True
        ).astype(jnp.float32)

    def to_heads(value):
        split = value.reshape(groups, count, part, -1).transpose(1, 0, 2, 3)
        return rows_to_frames(split.reshape(count, groups * part, -1), positions)

    resid_bf = delayed(frames, offsets).astype(jnp.bfloat16)
    resid_in = rows_to_positions(resid_bf).astype(jnp.float32)
    cot_own = rows_to_positions(cotangent)
    unit_one, scale_one, normed_one = normalize(resid_in, attn_gain)
    group_norm = flat(both(normed_one))
    group_cot = flat(both(cot_own))
    full_qkv = weights_to_positions(w_qkv).transpose(1, 0, 2, 3).reshape(3, width, heads_width)
    full_out = weights_to_positions(w_out.transpose(0, 2, 1)).reshape(width, heads_width)
    full_gate = weights_to_positions(w_gu[:, 0]).reshape(width, units)
    full_up = weights_to_positions(w_gu[:, 1]).reshape(width, units)
    full_down = weights_to_positions(w_down.transpose(0, 2, 1)).reshape(width, units)

    qkv_pos = matmul(group_norm, full_qkv, "xd,jde->xje").astype(jnp.bfloat16)
    qkv_low = to_heads(qkv_pos).reshape(copies * groups * part, positions, 3, heads_width)
    mixed_low, log_total = attend(qkv_low, HD)

    def frames_to_rows(value):
        moved = rows_to_positions(value)
        split = moved.reshape(count, groups, part, -1).transpose(1, 0, 2, 3)
        return split.reshape(groups * count * part, -1)

    mixed_pos = frames_to_rows(mixed_low)
    attn_sum = own_sum(matmul(mixed_pos, full_out, "xe,de->xd"))
    hidden_in = resid_in + attn_sum
    unit_two, scale_two, normed_two = normalize(hidden_in, ffn_gain)
    group_two = flat(both(normed_two))
    gate_pre = matmul(group_two, full_gate, "xd,de->xe")
    up_pre = matmul(group_two, full_up, "xd,de->xe")
    sigmoid_gate = jax.nn.sigmoid(gate_pre)
    silu_gate = gate_pre * sigmoid_gate
    hidden_low = (silu_gate * up_pre).astype(jnp.bfloat16)
    ffn_sum = own_sum(matmul(hidden_low, full_down, "xe,de->xd").astype(jnp.bfloat16))
    result = rows_to_frames((hidden_in + ffn_sum).astype(jnp.bfloat16), positions)

    grad_down = matmul(group_cot, hidden_low, "xd,xe->de")
    grad_hidden = matmul(group_cot, full_down, "xd,de->xe")
    slope = sigmoid_gate * (1.0 + gate_pre * (1.0 - sigmoid_gate))
    grad_gate = (grad_hidden * up_pre * slope).astype(jnp.bfloat16)
    grad_up = (grad_hidden * silu_gate).astype(jnp.bfloat16)
    grad_wgate = matmul(group_two, grad_gate, "xd,xe->de")
    grad_wup = matmul(group_two, grad_up, "xd,xe->de")
    grad_normed_two = own_sum(
        (
            matmul(grad_gate, full_gate, "xe,de->xd") + matmul(grad_up, full_up, "xe,de->xd")
        ).astype(jnp.bfloat16)
    )
    moved_down = swap(grad_down.reshape(count, -1, units).astype(jnp.bfloat16))
    back_two, gain_two = norm_back(grad_normed_two, unit_two, scale_two, ffn_gain)
    grad_hidden_in = cot_own.astype(jnp.float32) + back_two
    group_grad = flat(both(grad_hidden_in.astype(jnp.bfloat16)))
    grad_wout = matmul(group_grad, mixed_pos, "xd,xe->de")
    grad_mixed = matmul(group_grad, full_out, "xd,de->xe").astype(jnp.bfloat16)
    grad_mixed, moved_down = lax.optimization_barrier((grad_mixed, moved_down))
    grad_mixed_low = to_heads(grad_mixed)
    grad_qkv_low = attend_back(qkv_low, grad_mixed_low, log_total, HD)
    grad_qkv = frames_to_rows(
        grad_qkv_low.reshape(copies * groups * part, positions, 3 * heads_width)
    ).reshape(-1, 3, heads_width)
    grad_wqkv = matmul(group_norm, grad_qkv, "xd,xje->jde")
    grad_normed_one = own_sum(matmul(grad_qkv, full_qkv, "xje,jde->xd").astype(jnp.bfloat16))
    back_one, gain_one = norm_back(grad_normed_one, unit_one, scale_one, attn_gain)
    grad_resid = rows_to_frames((grad_hidden_in + back_one).astype(jnp.bfloat16), positions).astype(
        jnp.float32
    )
    one_step = jnp.where((offsets == 1)[:, :, None], grad_resid, 0.0)
    two_step = jnp.where((offsets == 2)[:, :, None], grad_resid, 0.0)
    spread = jnp.pad(one_step, ((1, 1), (0, 0), (0, 0))) + jnp.pad(
        two_step, ((0, 2), (0, 0), (0, 0))
    )
    returned = from_behind(spread[:2].astype(jnp.bfloat16), ("dp", "mp"), -1).astype(jnp.float32)
    grad_frames = (spread[2:] + jnp.pad(returned, ((row_count - 2, 0), (0, 0), (0, 0)))).astype(
        jnp.bfloat16
    )
    gains = jnp.stack([jnp.sum(gain_one, axis=0), jnp.sum(gain_two, axis=0)])
    gains = gains.reshape(2, count, groups, width // (count * groups))
    gains = lax.psum_scatter(
        gains.transpose(2, 1, 0, 3), "mp", scatter_dimension=0, tiled=False
    )
    gains = swap(gains)
    gains = jnp.sum(gains.reshape(positions, copies, 2, -1), axis=1)

    def split_rows(value):
        stacked = value.shape[0]
        return value.reshape(stacked, count, width // count, -1).transpose(1, 0, 2, 3)

    shard_qkv = grads_to_shards(split_rows(grad_wqkv), positions)
    shard_out = grads_to_shards(grad_wout.reshape(count, -1, heads_width), positions)
    shard_gate = grads_to_shards(grad_wgate.reshape(count, -1, units), positions)
    shard_up = grads_to_shards(grad_wup.reshape(count, -1, units), positions)
    shard_gu = jnp.stack([shard_gate, shard_up], axis=1)
    shard_down = sum_arrived(moved_down, positions)
    return (
        result,
        grad_frames,
        gains[:, 0],
        shard_qkv,
        shard_out.transpose(0, 2, 1),
        gains[:, 1],
        shard_gu,
        shard_down.transpose(0, 2, 1),
    )


def solution(mesh):
    return jax.shard_map(
        body,
        mesh=mesh,
        in_specs=(
            P(("dp", "mp"), None, None),
            P(("dp", "mp"), None),
            P(),
            P(None, None, "dp", "mp"),
            P(None, "mp", "dp"),
            P(),
            P(None, None, "dp", "mp"),
            P(None, "mp", "dp"),
            P(("dp", "mp"), None, None),
        ),
        out_specs=(
            P(("dp", "mp"), None, None),
            P(("dp", "mp"), None, None),
            P(None, ("dp", "mp")),
            P(None, None, "dp", "mp"),
            P(None, "mp", "dp"),
            P(None, ("dp", "mp")),
            P(None, None, "dp", "mp"),
            P(None, "mp", "dp"),
        ),
        check_vma=False,
    )
```
